32 devices in a mesh: parts: 2 (over y), samp: 4 (over x, core), bond: 4 (over z).
Axes of the slice: x: 2, y: 2, z: 4, core: 2. Of those that a mesh axis runs over, the one named last changes fastest.
Arguments:
- env_start: bfloat16 [4096, 4096], P(('parts', 'samp'), 'bond'), parts along dimension 0, may hold values from -6 to 6
- stored_sites: bfloat16 [4, 4, 1024, 4, 4096], P('parts', 'samp', None, None, 'bond'), parts along dimension 0, may hold values from -1 to 1
- slab_order: int32 [4, 4], P('parts'), parts along dimension 0, may hold values from 0 to 3, each once within a row
- chosen: int32 [4096, 2], P(('parts', 'samp')), parts along dimension 0, may hold values from 0 to 3
Outputs:
- probabilities: float32 [4096, 2, 4], P(('parts', 'samp')), parts along dimension 0
- env_final: float32 [4096, 4096], P(('parts', 'samp'), 'bond'), parts along dimension 0
The draws below stay inside these ranges and needn't reach their ends.
There are 2 independent parts, one for each index of `parts`. The reference program is written for one: setup_inputs(seed, part) draws one part's arguments, and reference() takes and returns one part's arrays. A program takes and returns all parts, laid end to end along the dimension named above; each array names one. Nothing has to cross between parts.
Inputs may be any that keep to these rules, and one draw needn't show every extreme that they name: Each row of slab_order names every index of samp once.
All inputs are finite; a program needn't handle non-finite values.
Results may differ from the reference program's by a relative error of at most 0.005.
Values may be sent and summed in bfloat16 or wider, within the bound.
A program may use at most 192 MiB of HBM per device.

```python
import math
import jax
import jax.numpy as jnp
from jax import lax

CHI = 4096
D_F = 4
STEPS = 2
SAMPLES = 2048
SLAB = 1024
N_SAMP = 4


def draw_stored_sites(key, part):
    key_base = jax.random.fold_in(key, 11)
    key_cols = jax.random.fold_in(key, 12)
    base = jnp.clip(jax.random.normal(key_base, (STEPS, N_SAMP, SLAB, D_F, CHI), jnp.float32), -6.0, 6.0)
    position = jnp.arange(CHI, dtype=jnp.float32) / max(CHI - 1, 1)
    col_scale = jnp.exp(jax.random.uniform(key_cols, (CHI,), jnp.float32, 0.0, math.log(10.0)))
    col_scale = col_scale * jnp.exp(0.5 * math.log(3.0) * position)
    scaled = base * col_scale / (4.0 * math.sqrt(CHI))
    return jnp.clip(scaled, -1.0, 1.0).astype(jnp.bfloat16)


def with_ends(values, own_key, least, top_value):
    dims = values.shape
    spot = [jax.random.randint(jax.random.fold_in(own_key, axis), (), 0, dims[axis]) for axis in range(len(dims))]
    values = values.at[tuple(spot)].set(least)
    longest = dims.index(max(dims))
    spot[longest] = (spot[longest] + 1) % dims[longest]
    return values.at[tuple(spot)].set(top_value)


def shard_levels(own_key, shape, cuts, smallest, top_value):
    gain, own = 1.0, jax.random.fold_in(own_key, 6)
    for axis_at, parts in cuts:
        draws = jnp.exp(jax.random.uniform(jax.random.fold_in(own, axis_at), (parts,), jnp.float32, smallest / len(cuts), top_value / len(cuts)))
        gain = gain * jnp.repeat(draws, shape[axis_at] // parts).reshape([-1 if axis == axis_at else 1 for axis in range(len(shape))])
    return gain


def gaussian(rng, extent, spread, most, pieces=(), kind=jnp.bfloat16):
    level = shard_levels(rng, extent, pieces, -0.22, 0.18) if pieces else 1.0
    drawn = jax.random.normal(rng, extent, jnp.float32) * spread * level
    return jnp.minimum(jnp.maximum(drawn, -most), most).astype(kind)


def setup_inputs(seed: int = 0, part: int = 0) -> dict:
    key_of = jax.random.split(jax.random.key(seed), 5)
    part_keys = jax.random.split(jax.random.fold_in(key_of[4], part), 5)
    return {
        "env_start": gaussian(part_keys[0], (SAMPLES, CHI), 1.0, 6.0, ((0, 4), (1, 4))),
        "stored_sites": draw_stored_sites(jax.random.fold_in(jax.random.fold_in(key_of[4], part), 71), part),
        "slab_order": jax.vmap(lambda own: jax.random.permutation(own, N_SAMP))(jax.random.split(part_keys[2], STEPS)).reshape((STEPS, N_SAMP)).astype(jnp.int32),
        "chosen": with_ends(jax.random.randint(part_keys[3], (SAMPLES, STEPS), 0, D_F), jax.random.fold_in(part_keys[3], 1), 0, D_F - 1).astype(jnp.int32),
    }


epsilon = 1e-06

def reference(env_start, stored_sites, slab_order, chosen):
    samples = env_start.shape[0]
    raw_env = env_start
    factor = jnp.ones((samples,), jnp.float32)
    outcomes = jnp.arange(D_F, dtype=jnp.int32)
    prob_list = []
    selected = None
    for site_index in range(STEPS):
        blocks = raw_env.reshape(samples, N_SAMP, SLAB)
        ordered = jnp.take(blocks, slab_order[site_index].astype(jnp.int32), axis=1).reshape(samples, CHI)
        site_block = stored_sites[site_index].reshape(CHI, D_F * CHI)
        product = jnp.dot(ordered, site_block, preferred_element_type=jnp.float32).reshape(samples, D_F, CHI)
        amplitude = product * factor[:, None, None]
        totals = lax.optimization_barrier(jnp.sum(amplitude * amplitude, axis=2))
        prob_list.append(totals / lax.optimization_barrier(jnp.sum(totals, axis=1, keepdims=True)))
        selector = (chosen[:, site_index][:, None] == outcomes[None, :]).astype(jnp.float32)
        selected = jnp.einsum('sn,snc->sc', selector, product)
        chosen_total = lax.optimization_barrier(jnp.sum(totals * selector, axis=1))
        factor = factor * lax.rsqrt(chosen_total / CHI + epsilon)
        if site_index + 1 < STEPS:
            raw_env = selected.astype(jnp.bfloat16)
    env_final = selected * factor[:, None]
    return (jnp.stack(prob_list, axis=1), env_final)
```

```python
import functools

import jax
import jax.numpy as jnp
from jax import lax
from jax.experimental import pallas as pl
from jax.experimental.pallas import tpu as pltpu
from jax.sharding import PartitionSpec as P

STEPS = 2
CHUNKS = 4
epsilon = 1e-06


def tile_of(width):
    return min(width, 256)


def weight_specs(weights, tile):
    return [pl.BlockSpec((w.shape[0], w.shape[1], tile), lambda t: (0, 0, t)) for w in weights]


def dots(env_ref, weight_refs, outcome):
    total = None
    for part, weight_ref in enumerate(weight_refs):
        term = jnp.dot(env_ref[part], weight_ref[outcome], preferred_element_type=jnp.float32)
        total = term if total is None else total + term
    return total


def cost(env, weights):
    flops = 2 * env.shape[1] * sum(w.size for w in weights)
    return pl.CostEstimate(flops=flops, bytes_accessed=2 * sum(w.size for w in weights), transcendentals=0)


def partial_kernel(count, env_ref, *refs):
    weight_refs, out_ref = refs[:count], refs[count]
    for outcome in range(out_ref.shape[0]):
        out_ref[outcome] = dots(env_ref, weight_refs, outcome).astype(out_ref.dtype)


def partial_product(env, weights):
    outcomes, _, width = weights[0].shape
    samples, tile = env.shape[1], tile_of(width)
    return pl.pallas_call(
        functools.partial(partial_kernel, len(weights)),
        grid=(width // tile,),
        in_specs=[pl.BlockSpec(env.shape, lambda t: (0, 0, 0))] + weight_specs(weights, tile),
        out_specs=pl.BlockSpec((outcomes, samples, tile), lambda t: (0, 0, t)),
        out_shape=jax.ShapeDtypeStruct((outcomes, samples, width), jnp.bfloat16),
        cost_estimate=cost(env, weights),
    )(env, *weights)


def finish_kernel(count, others, env_ref, chosen_ref, *refs):
    weight_refs, other_refs = refs[:count], refs[count : count + others]
    totals_ref, selected_ref = refs[count + others :]

    @pl.when(pl.program_id(0) == 0)
    def _():
        totals_ref[...] = jnp.zeros_like(totals_ref)

    lane = lax.broadcasted_iota(jnp.int32, totals_ref.shape, 1)
    selected = None
    added = jnp.zeros(totals_ref.shape, jnp.float32)
    for outcome in range(weight_refs[0].shape[0]):
        total = dots(env_ref, weight_refs, outcome)
        for other_ref in other_refs:
            total = total + other_ref[outcome].astype(jnp.float32)
        norm = jnp.sum(total * total, axis=1, keepdims=True)
        added = jnp.where(lane == outcome, norm, added)
        hit = chosen_ref[...] == outcome
        selected = jnp.where(hit, total, 0.0 if selected is None else selected)
    totals_ref[...] += added
    selected_ref[...] = selected.astype(selected_ref.dtype)


def finish_product(env, weights, others, chosen, dtype):
    outcomes, _, width = weights[0].shape
    samples, tile = env.shape[1], tile_of(width)
    return pl.pallas_call(
        functools.partial(finish_kernel, len(weights), len(others)),
        grid=(width // tile,),
        in_specs=[
            pl.BlockSpec(env.shape, lambda t: (0, 0, 0)),
            pl.BlockSpec((samples, 1), lambda t: (0, 0)),
        ]
        + weight_specs(weights, tile)
        + [pl.BlockSpec((outcomes, samples, tile), lambda t: (0, 0, t)) for _ in others],
        out_specs=(
            pl.BlockSpec((samples, 128), lambda t: (0, 0)),
            pl.BlockSpec((samples, tile), lambda t: (0, t)),
        ),
        out_shape=(
            jax.ShapeDtypeStruct((samples, 128), jnp.float32),
            jax.ShapeDtypeStruct((samples, width), dtype),
        ),
        cost_estimate=cost(env, weights),
    )(env, chosen, *weights, *others)


def body(env_start, stored_sites, slab_order, chosen):
    groups = slab_order.shape[1]
    inner = 2 if groups % 2 == 0 else 1
    outer = groups // inner
    bonds = lax.axis_size("bond")
    mine, place = lax.axis_index("samp"), lax.axis_index("bond")
    core, chip = mine % inner, mine // inner
    rows, outcomes, width = stored_sites.shape[2:]
    bond_width = width * bonds
    samples = env_start.shape[0]
    chunks = CHUNKS if samples % (CHUNKS * 16) == 0 else 1
    size = samples // chunks

    def across(value, step):
        return lax.ppermute(
            value, "samp", [(i, ((i // inner + step) % outer) * inner + i % inner) for i in range(groups)]
        )

    def inside(value, step):
        return lax.ppermute(
            value, "samp", [((i // inner) * inner + (i + step) % inner, i) for i in range(groups)]
        )

    def along(value, step):
        return lax.ppermute(value, "bond", [(i, (i + step) % bonds) for i in range(bonds)])

    weights = []
    for site in range(STEPS):
        own = jnp.transpose(stored_sites[site, 0], (1, 0, 2))
        weights.append([own] + [inside(own, step) for step in range(1, inner)])

    def gather(value):
        if bonds == groups:
            pieces = jnp.stack([value] + [along(value, step) for step in range(1, bonds)])
            return lambda block: lax.dynamic_index_in_dim(
                pieces, (place - block + bonds) % bonds, 0, keepdims=False
            )
        whole = lax.all_gather(value, "bond", axis=1, tiled=True)
        return lambda block: lax.dynamic_slice_in_dim(whole, block * rows, rows, axis=1)

    def blocks_for(pick, site, target):
        return jnp.stack(
            [pick(slab_order[site, target * inner + (core + step) % inner]) for step in range(inner)]
        )

    def bond_sum(value):
        if bonds <= 4:
            return sum([along(value, step) for step in range(1, bonds)], value)
        return lax.psum(value, "bond")

    raws = [env_start[c * size : (c + 1) * size] for c in range(chunks)]
    picks = [chosen[c * size : (c + 1) * size] for c in range(chunks)]
    totals = []
    for site in range(STEPS):
        last = site + 1 == STEPS
        site_totals = []
        for c in range(chunks):
            pick = gather(raws[c])
            others = []
            for step in range(1, outer):
                foreign = across(blocks_for(pick, site, (chip + step) % outer), step)
                others.append(across(partial_product(foreign, weights[site]), -step))
            norms, raws[c] = finish_product(
                blocks_for(pick, site, chip),
                weights[site],
                others,
                picks[c][:, site : site + 1],
                jnp.float32 if last else jnp.bfloat16,
            )
            site_totals.append(bond_sum(norms)[:, :outcomes])
        totals.append(site_totals)
    probabilities, finals = [], []
    labels = jnp.arange(outcomes, dtype=jnp.int32)
    for c in range(chunks):
        factor = jnp.ones((size,), jnp.float32)
        rows_out = []
        for site in range(STEPS):
            scaled = totals[site][c] * (factor * factor)[:, None]
            rows_out.append(scaled / jnp.sum(scaled, axis=1, keepdims=True))
            hit = picks[c][:, site][:, None] == labels[None, :]
            factor = factor * lax.rsqrt(jnp.sum(jnp.where(hit, scaled, 0.0), axis=1) / bond_width + epsilon)
        probabilities.append(jnp.stack(rows_out, axis=1))
        finals.append(raws[c] * factor[:, None])
    return jnp.concatenate(probabilities), jnp.concatenate(finals)


def solution(mesh):
    return jax.shard_map(
        body,
        mesh=mesh,
        in_specs=(
            P(("parts", "samp"), "bond"),
            P("parts", "samp", None, None, "bond"),
            P("parts", None),
            P(("parts", "samp"), None),
        ),
        out_specs=(P(("parts", "samp"), None, None), P(("parts", "samp"), "bond")),
        check_vma=False,
    )
```

```python
import functools

import jax
import jax.numpy as jnp
from jax import lax
from jax.experimental import pallas as pl
from jax.experimental.pallas import tpu as pltpu
from jax.sharding import PartitionSpec as P


STEPS = 2
CHUNKS = 2
epsilon = 1e-06


def tile_of(width):
    return min(width, 256)


def weight_specs(weights, tile):
    return [pl.BlockSpec((w.shape[0], w.shape[1], tile), lambda t: (0, 0, t)) for w in weights]


def dots(env_ref, weight_refs, outcome):
    total = None
    for part, weight_ref in enumerate(weight_refs):
        term = jnp.dot(env_ref[part], weight_ref[outcome], preferred_element_type=jnp.float32)
        total = term if total is None else total + term
    return total


def cost(env, weights):
    flops = 2 * env.shape[1] * sum(w.size for w in weights)
    return pl.CostEstimate(flops=flops, bytes_accessed=2 * sum(w.size for w in weights), transcendentals=0)


def partial_kernel(count, env_ref, *refs):
    weight_refs, out_ref = refs[:count], refs[count]
    for outcome in range(out_ref.shape[0]):
        out_ref[outcome] = dots(env_ref, weight_refs, outcome).astype(out_ref.dtype)


def partial_product(env, weights):
    outcomes, _, width = weights[0].shape
    samples, tile = env.shape[1], tile_of(width)
    return pl.pallas_call(
        functools.partial(partial_kernel, len(weights)),
        grid=(width // tile,),
        in_specs=[pl.BlockSpec(env.shape, lambda t: (0, 0, 0))] + weight_specs(weights, tile),
        out_specs=pl.BlockSpec((outcomes, samples, tile), lambda t: (0, 0, t)),
        out_shape=jax.ShapeDtypeStruct((outcomes, samples, width), jnp.bfloat16),
        cost_estimate=cost(env, weights),
    )(env, *weights)


def finish_kernel(count, others, site, env_ref, chosen_ref, before_ref, *refs):
    weight_refs, other_refs = refs[:count], refs[count : count + others]
    totals_ref, selected_ref = refs[count + others :]
    outcomes = weight_refs[0].shape[0]

    @pl.when(pl.program_id(0) == 0)
    def _():
        totals_ref[...] = before_ref[...]

    lane = lax.broadcasted_iota(jnp.int32, totals_ref.shape, 1)
    selected = None
    added = jnp.zeros(totals_ref.shape, jnp.float32)
    for outcome in range(outcomes):
        total = dots(env_ref, weight_refs, outcome)
        for other_ref in other_refs:
            total = total + other_ref[outcome].astype(jnp.float32)
        norm = jnp.sum(total * total, axis=1, keepdims=True)
        added = jnp.where(lane == site * outcomes + outcome, norm, added)
        hit = chosen_ref[...] == outcome
        selected = jnp.where(hit, total, 0.0 if selected is None else selected)
    totals_ref[...] += added
    selected_ref[...] = selected.astype(selected_ref.dtype)


def finish_product(env, weights, others, chosen, before, site, dtype):
    outcomes, _, width = weights[0].shape
    samples, tile = env.shape[1], tile_of(width)
    return pl.pallas_call(
        functools.partial(finish_kernel, len(weights), len(others), site),
        grid=(width // tile,),
        in_specs=[
            pl.BlockSpec(env.shape, lambda t: (0, 0, 0)),
            pl.BlockSpec((samples, 1), lambda t: (0, 0)),
            pl.BlockSpec((samples, 128), lambda t: (0, 0)),
        ]
        + weight_specs(weights, tile)
        + [pl.BlockSpec((outcomes, samples, tile), lambda t: (0, 0, t)) for _ in others],
        out_specs=(
            pl.BlockSpec((samples, 128), lambda t: (0, 0)),
            pl.BlockSpec((samples, tile), lambda t: (0, t)),
        ),
        out_shape=(
            jax.ShapeDtypeStruct((samples, 128), jnp.float32),
            jax.ShapeDtypeStruct((samples, width), dtype),
        ),
        cost_estimate=cost(env, weights),
    )(env, chosen, before, *weights, *others)


def relayout_kernel(stored_ref, _, out_ref):
    for outcome in range(out_ref.shape[0]):
        out_ref[outcome] = stored_ref[0, 0, :, outcome, :]


def relayout(stored_sites, site, after):
    rows, outcomes, width = stored_sites.shape[2:]
    tile = min(rows, 128)
    return pl.pallas_call(
        relayout_kernel,
        grid=(rows // tile,),
        in_specs=[
            pl.BlockSpec((1, 1, tile, outcomes, width), lambda t: (site, 0, t, 0, 0)),
            pl.BlockSpec(memory_space=pl.ANY),
        ],
        out_specs=pl.BlockSpec((outcomes, tile, width), lambda t: (0, t, 0)),
        out_shape=jax.ShapeDtypeStruct((outcomes, rows, width), stored_sites.dtype),
        cost_estimate=pl.CostEstimate(
            flops=0, bytes_accessed=4 * rows * outcomes * width, transcendentals=0
        ),
    )(stored_sites, after)


def pick_kernel(inner, index_ref, *refs):
    pieces, outs = refs[: len(refs) - inner[1]], refs[len(refs) - inner[1] :]
    for target, out_ref in enumerate(outs):
        for part in range(inner[0]):
            for source, piece_ref in enumerate(pieces):

                @pl.when(index_ref[target * inner[0] + part] == source)
                def _():
                    out_ref[part] = piece_ref[...]


def pick_blocks(index, pieces, outer, inner):
    samples, width = pieces[0].shape
    spec = pl.BlockSpec((samples, width), lambda t, index: (0, 0))
    return pl.pallas_call(
        functools.partial(pick_kernel, (inner, outer)),
        grid_spec=pltpu.PrefetchScalarGridSpec(
            num_scalar_prefetch=1,
            grid=(1,),
            in_specs=[spec] * len(pieces),
            out_specs=[pl.BlockSpec((inner, samples, width), lambda t, index: (0, 0, 0))] * outer,
        ),
        out_shape=[jax.ShapeDtypeStruct((inner, samples, width), pieces[0].dtype)] * outer,
        cost_estimate=pl.CostEstimate(
            flops=0, bytes_accessed=2 * samples * width * (len(pieces) + outer * inner), transcendentals=0
        ),
    )(index, *pieces)


def compute(env_start, stored_sites, slab_order, chosen):
    groups = slab_order.shape[1]
    inner = 2 if groups % 2 == 0 else 1
    outer = groups // inner
    bonds = lax.axis_size("bond")
    mine, place = lax.axis_index("samp"), lax.axis_index("bond")
    core, chip = mine % inner, mine // inner
    rows, outcomes, width = stored_sites.shape[2:]
    bond_width = width * bonds
    samples = env_start.shape[0]
    chunks = CHUNKS if samples % (CHUNKS * 16) == 0 else 1
    size = samples // chunks

    def across(value, step):
        return lax.ppermute(
            value, "samp", [(i, ((i // inner + step) % outer) * inner + i % inner) for i in range(groups)]
        )

    def inside(value, step):
        return lax.ppermute(
            value, "samp", [((i // inner) * inner + (i + step) % inner, i) for i in range(groups)]
        )

    def along(value, step):
        return lax.ppermute(value, "bond", [(i, (i + step) % bonds) for i in range(bonds)])

    def load(site, after):
        own = relayout(stored_sites, site, after)
        return [own] + [inside(own, step) for step in range(1, inner)]

    wanted = [
        jnp.stack(
            [
                slab_order[site, ((chip + step) % outer) * inner + (core + part) % inner]
                for step in range(outer)
                for part in range(inner)
            ]
        )
        for site in range(STEPS)
    ]

    def gather(value, site):
        if bonds == groups:
            pieces = [value] + [along(value, step) for step in range(1, bonds)]
            index = (place - wanted[site] + bonds) % bonds
            return lambda: pick_blocks(index, pieces, outer, inner)
        whole = lax.all_gather(value, "bond", axis=1, tiled=True)
        blocks = [
            lax.dynamic_slice_in_dim(whole, wanted[site][i] * rows, rows, axis=1)
            for i in range(groups)
        ]
        return lambda: [
            jnp.stack(blocks[step * inner : (step + 1) * inner]) for step in range(outer)
        ]

    def bond_sum(value):
        if bonds <= 4:
            return sum([along(value, step) for step in range(1, bonds)], value)
        return lax.psum(value, "bond")

    raws = [env_start[c * size : (c + 1) * size] for c in range(chunks)]
    picks = [chosen[c * size : (c + 1) * size] for c in range(chunks)]
    norms = [jnp.zeros((size, 128), jnp.float32)] * chunks

    def fetch(value, site):
        pick = gather(value, site)
        own, *foreign = pick()
        return own, [(i + 1, across(block, i + 1)) for i, block in enumerate(foreign)]

    owns, sents = [], []
    for c in range(chunks):
        own, sent = fetch(raws[c], 0)
        owns.append(own)
        sents.append(sent)
    weights = load(0, norms[0])
    for site in range(STEPS):
        last = site + 1 == STEPS
        answers = []
        for c in range(chunks):
            partials = [(step, partial_product(foreign, weights)) for step, foreign in sents[c]]
            if c == 0 and not last:
                later = load(site + 1, partials[0][1] if partials else norms[0])
            answers.append([across(value, -step) for step, value in partials])
        new_owns, new_sents = [], []
        for c in range(chunks):
            norms[c], raws[c] = finish_product(
                owns[c],
                weights,
                answers[c],
                picks[c][:, site : site + 1],
                norms[c],
                site,
                jnp.float32 if last else jnp.bfloat16,
            )
            if not last:
                own, sent = fetch(raws[c], site + 1)
                new_owns.append(own)
                new_sents.append(sent)
        if not last:
            owns, sents, weights = new_owns, new_sents, later
    sums = [bond_sum(norm) for norm in norms]
    totals = [[s[:, site * outcomes : (site + 1) * outcomes] for s in sums] for site in range(STEPS)]
    probabilities, finals = [], []
    labels = jnp.arange(outcomes, dtype=jnp.int32)
    for c in range(chunks):
        factor = jnp.ones((size,), jnp.float32)
        rows_out = []
        for site in range(STEPS):
            scaled = totals[site][c] * (factor * factor)[:, None]
            rows_out.append(scaled / jnp.sum(scaled, axis=1, keepdims=True))
            hit = picks[c][:, site][:, None] == labels[None, :]
            factor = factor * lax.rsqrt(jnp.sum(jnp.where(hit, scaled, 0.0), axis=1) / bond_width + epsilon)
        probabilities.append(jnp.stack(rows_out, axis=1))
        finals.append(raws[c] * factor[:, None])
    return jnp.concatenate(probabilities), jnp.concatenate(finals)


def solution(mesh):
    return jax.shard_map(
        compute,
        mesh=mesh,
        in_specs=(
            P(("parts", "samp"), "bond"),
            P("parts", "samp", None, None, "bond"),
            P("parts", None),
            P(("parts", "samp"), None),
        ),
        out_specs=(P(("parts", "samp"), None, None), P(("parts", "samp"), "bond")),
        check_vma=False,
    )
```

```python
import functools

import jax
import jax.numpy as jnp
from jax import lax
from jax.experimental import pallas as pl
from jax.experimental.pallas import tpu as pltpu
from jax.sharding import PartitionSpec as P


STEPS = 2
CHUNKS = 2
PIECES = 2
epsilon = 1e-06


def tile_of(width):
    return min(width, 256)


def dots(env_ref, weight_refs, outcome):
    total = None
    for part, weight_ref in enumerate(weight_refs):
        term = jnp.dot(env_ref[part], weight_ref[outcome], preferred_element_type=jnp.float32)
        total = term if total is None else total + term
    return total


def product_kernel(count, env_ref, *refs):
    weight_refs, out_ref = refs[:count], refs[count]
    for outcome in range(out_ref.shape[0]):
        out_ref[outcome] = dots(env_ref, weight_refs, outcome).astype(out_ref.dtype)


def product(env, weights, piece, pieces, dtype):
    outcomes, rows, width = weights[0].shape
    count = outcomes // pieces
    samples, tile = env.shape[1], tile_of(width)
    flops = 2 * samples * sum(w.size for w in weights) // pieces
    moved = 2 * sum(w.size for w in weights) // pieces
    return pl.pallas_call(
        functools.partial(product_kernel, len(weights)),
        grid=(width // tile,),
        in_specs=[pl.BlockSpec(env.shape, lambda t: (0, 0, 0))]
        + [pl.BlockSpec((count, rows, tile), lambda t: (piece, 0, t)) for _ in weights],
        out_specs=pl.BlockSpec((count, samples, tile), lambda t: (0, 0, t)),
        out_shape=jax.ShapeDtypeStruct((count, samples, width), dtype),
        cost_estimate=pl.CostEstimate(flops=flops, bytes_accessed=moved, transcendentals=0),
    )(env, *weights)


def finish_kernel(pieces, site, own_ref, chosen_ref, before_ref, *refs):
    other_refs, (totals_ref, selected_ref) = refs[:-2], refs[-2:]
    outcomes = own_ref.shape[0]
    each = outcomes // pieces

    @pl.when(pl.program_id(0) == 0)
    def _():
        totals_ref[...] = before_ref[...]

    lane = lax.broadcasted_iota(jnp.int32, totals_ref.shape, 1)
    selected = None
    added = jnp.zeros(totals_ref.shape, jnp.float32)
    for outcome in range(outcomes):
        total = own_ref[outcome]
        for other_ref in other_refs[outcome // each :: pieces]:
            total = total + other_ref[outcome % each].astype(jnp.float32)
        norm = jnp.sum(total * total, axis=1, keepdims=True)
        added = jnp.where(lane == site * outcomes + outcome, norm, added)
        hit = chosen_ref[...] == outcome
        selected = jnp.where(hit, total, 0.0 if selected is None else selected)
    totals_ref[...] += added
    selected_ref[...] = selected.astype(selected_ref.dtype)


def finish(own, others, chosen, before, site, dtype):
    outcomes, samples, width = own.shape
    tile = tile_of(width)
    pieces = outcomes // others[0].shape[0] if others else 1
    return pl.pallas_call(
        functools.partial(finish_kernel, pieces, site),
        grid=(width // tile,),
        in_specs=[
            pl.BlockSpec((outcomes, samples, tile), lambda t: (0, 0, t)),
            pl.BlockSpec((samples, 1), lambda t: (0, 0)),
            pl.BlockSpec((samples, 128), lambda t: (0, 0)),
        ]
        + [pl.BlockSpec((outcomes // pieces, samples, tile), lambda t: (0, 0, t)) for _ in others],
        out_specs=(
            pl.BlockSpec((samples, 128), lambda t: (0, 0)),
            pl.BlockSpec((samples, tile), lambda t: (0, t)),
        ),
        out_shape=(
            jax.ShapeDtypeStruct((samples, 128), jnp.float32),
            jax.ShapeDtypeStruct((samples, width), dtype),
        ),
        cost_estimate=pl.CostEstimate(
            flops=4 * own.size, bytes_accessed=8 * own.size, transcendentals=0
        ),
    )(own, chosen, before, *others)


def relayout_kernel(stored_ref, _, out_ref):
    for outcome in range(out_ref.shape[0]):
        out_ref[outcome] = stored_ref[0, 0, :, outcome, :]


def relayout(stored_sites, site, after):
    rows, outcomes, width = stored_sites.shape[2:]
    tile = min(rows, 128)
    return pl.pallas_call(
        relayout_kernel,
        grid=(rows // tile,),
        in_specs=[
            pl.BlockSpec((1, 1, tile, outcomes, width), lambda t: (site, 0, t, 0, 0)),
            pl.BlockSpec(memory_space=pl.ANY),
        ],
        out_specs=pl.BlockSpec((outcomes, tile, width), lambda t: (0, t, 0)),
        out_shape=jax.ShapeDtypeStruct((outcomes, rows, width), stored_sites.dtype),
        cost_estimate=pl.CostEstimate(
            flops=0, bytes_accessed=4 * rows * outcomes * width, transcendentals=0
        ),
    )(stored_sites, after)


def pick_kernel(inner, index_ref, *refs):
    pieces, outs = refs[: len(refs) - inner[1]], refs[len(refs) - inner[1] :]
    for target, out_ref in enumerate(outs):
        for part in range(inner[0]):
            for source, piece_ref in enumerate(pieces):

                @pl.when(index_ref[target * inner[0] + part] == source)
                def _():
                    out_ref[part] = piece_ref[...]


def pick_blocks(index, pieces, outer, inner):
    samples, width = pieces[0].shape
    spec = pl.BlockSpec((samples, width), lambda t, index: (0, 0))
    return pl.pallas_call(
        functools.partial(pick_kernel, (inner, outer)),
        grid_spec=pltpu.PrefetchScalarGridSpec(
            num_scalar_prefetch=1,
            grid=(1,),
            in_specs=[spec] * len(pieces),
            out_specs=[pl.BlockSpec((inner, samples, width), lambda t, index: (0, 0, 0))] * outer,
        ),
        out_shape=[jax.ShapeDtypeStruct((inner, samples, width), pieces[0].dtype)] * outer,
        cost_estimate=pl.CostEstimate(
            flops=0, bytes_accessed=2 * samples * width * (len(pieces) + outer * inner), transcendentals=0
        ),
    )(index, *pieces)


def compute(env_start, stored_sites, slab_order, chosen):
    groups = slab_order.shape[1]
    inner = 2 if groups % 2 == 0 else 1
    outer = groups // inner
    bonds = lax.axis_size("bond")
    mine, place = lax.axis_index("samp"), lax.axis_index("bond")
    core, chip = mine % inner, mine // inner
    rows, outcomes, width = stored_sites.shape[2:]
    bond_width = width * bonds
    samples = env_start.shape[0]
    chunks = CHUNKS if samples % (CHUNKS * 16) == 0 else 1
    size = samples // chunks

    def across(value, step):
        return lax.ppermute(
            value, "samp", [(i, ((i // inner + step) % outer) * inner + i % inner) for i in range(groups)]
        )

    def inside(value, step):
        return lax.ppermute(
            value, "samp", [((i // inner) * inner + (i + step) % inner, i) for i in range(groups)]
        )

    def along(value, step):
        return lax.ppermute(value, "bond", [(i, (i + step) % bonds) for i in range(bonds)])

    def load(site, after):
        own = relayout(stored_sites, site, after)
        return [own] + [inside(own, step) for step in range(1, inner)]

    wanted = [
        jnp.stack(
            [
                slab_order[site, ((chip + step) % outer) * inner + (core + part) % inner]
                for step in range(outer)
                for part in range(inner)
            ]
        )
        for site in range(STEPS)
    ]

    def gather(value, site):
        if bonds == groups:
            pieces = [value] + [along(value, step) for step in range(1, bonds)]
            index = (place - wanted[site] + bonds) % bonds
            return lambda: pick_blocks(index, pieces, outer, inner)
        whole = lax.all_gather(value, "bond", axis=1, tiled=True)
        blocks = [
            lax.dynamic_slice_in_dim(whole, wanted[site][i] * rows, rows, axis=1)
            for i in range(groups)
        ]
        return lambda: [
            jnp.stack(blocks[step * inner : (step + 1) * inner]) for step in range(outer)
        ]

    def bond_sum(value):
        if bonds <= 4:
            return sum([along(value, step) for step in range(1, bonds)], value)
        return lax.psum(value, "bond")

    raws = [env_start[c * size : (c + 1) * size] for c in range(chunks)]
    picks = [chosen[c * size : (c + 1) * size] for c in range(chunks)]
    norms = [jnp.zeros((size, 128), jnp.float32)] * chunks

    def fetch(value, site):
        pick = gather(value, site)
        own, *foreign = pick()
        return own, [(i + 1, across(block, i + 1)) for i, block in enumerate(foreign)]

    owns, sents = [], []
    for c in range(chunks):
        own, sent = fetch(raws[c], 0)
        owns.append(own)
        sents.append(sent)
    weights = load(0, norms[0])
    for site in range(STEPS):
        last = site + 1 == STEPS
        answers = []
        for c in range(chunks):
            parts, anchor = [], norms[0]
            for step, foreign in sents[c]:
                for piece in range(PIECES):
                    anchor = product(foreign, weights, piece, PIECES, jnp.bfloat16)
                    parts.append(across(anchor, -step))
            answers.append(parts)
            if c == 0 and not last:
                later = load(site + 1, anchor)
        new_owns, new_sents = [], []
        for c in range(chunks):
            own = product(owns[c], weights, 0, 1, jnp.float32)
            norms[c], raws[c] = finish(
                own,
                answers[c],
                picks[c][:, site : site + 1],
                norms[c],
                site,
                jnp.float32 if last else jnp.bfloat16,
            )
            if not last:
                own, sent = fetch(raws[c], site + 1)
                new_owns.append(own)
                new_sents.append(sent)
        if not last:
            owns, sents, weights = new_owns, new_sents, later
    sums = [bond_sum(norm) for norm in norms]
    totals = [[s[:, site * outcomes : (site + 1) * outcomes] for s in sums] for site in range(STEPS)]
    probabilities, finals = [], []
    labels = jnp.arange(outcomes, dtype=jnp.int32)
    for c in range(chunks):
        factor = jnp.ones((size,), jnp.float32)
        rows_out = []
        for site in range(STEPS):
            scaled = totals[site][c] * (factor * factor)[:, None]
            rows_out.append(scaled / jnp.sum(scaled, axis=1, keepdims=True))
            hit = picks[c][:, site][:, None] == labels[None, :]
            factor = factor * lax.rsqrt(jnp.sum(jnp.where(hit, scaled, 0.0), axis=1) / bond_width + epsilon)
        probabilities.append(jnp.stack(rows_out, axis=1))
        finals.append(raws[c] * factor[:, None])
    return jnp.concatenate(probabilities), jnp.concatenate(finals)


def solution(mesh):
    return jax.shard_map(
        compute,
        mesh=mesh,
        in_specs=(
            P(("parts", "samp"), "bond"),
            P("parts", "samp", None, None, "bond"),
            P("parts", None),
            P(("parts", "samp"), None),
        ),
        out_specs=(P(("parts", "samp"), None, None), P(("parts", "samp"), "bond")),
        check_vma=False,
    )
```
